32 devices in a mesh: groups: 2 (over y), slab: 4 (over z), coil: 2 (over x), pencil: 2 (over core).
Axes of the slice: x: 2, y: 2, z: 4, core: 2. Of those that a mesh axis runs over, the one named last changes fastest.
Arguments:
- estimate: float32 [2, 256, 128, 128], P(None, ('groups', 'slab', 'pencil'), 'coil'), parts along dimension 1, may hold values from -6 to 6
- coil_sens: bfloat16 [2, 8, 256, 128, 128], P(None, 'coil', ('groups', 'slab', 'pencil')), parts along dimension 2, may hold values from -3 to 3
- measured: bfloat16 [2, 8, 128, 256, 128], P(None, 'coil', None, ('groups', 'slab', 'pencil')), parts along dimension 3, may hold values from -4.1875 to 4.1875
- sampling: int32 [128, 256], P(None, ('groups', 'slab', 'pencil')), parts along dimension 1, may hold values 0 or 1
- step_size: float32 [1], replicated, may hold values from 0.2 to 2
- conv_in: bfloat16 [32, 2, 3, 3, 3], replicated, may hold values from -0.875 to 0.875
- bias_in: float32 [32], replicated, may hold values from -3 to 3
- conv_out: bfloat16 [2, 32, 3, 3, 3], replicated, may hold values from -0.21875 to 0.21875
Outputs:
- refined: float32 [2, 256, 128, 128], P(None, ('groups', 'slab', 'pencil'), 'coil'), parts along dimension 1
The draws below stay inside these ranges and needn't reach their ends.
There are 2 independent parts, one for each index of `groups`. The reference program is written for one: setup_inputs(seed, part) draws one part's arguments, and reference() takes and returns one part's arrays. A program takes and returns all parts, laid end to end along the dimension named above; an argument that names none is the same for every part. Nothing has to cross between parts.
All inputs are finite; a program needn't handle non-finite values. No bound on the sum of `sampling` on one device may be relied on, other than what follows from the above.
Results may differ from the reference program's by a relative error of at most 0.0014.
Values may be sent and summed in bfloat16 or wider, within the bound.
No kernel may reach another device: no remote copies, remote signals or barrier semaphores. Data moves between devices by JAX's collectives and lax.ppermute only.
A program may use at most 192 MiB of HBM per device.

```python
import jax
import jax.numpy as jnp
from jax import lax

NX = 128
NY = 128
NZ = 128
NCOIL = 8
HID = 32


def set_ends(array, own_key, smallest, high):
    dims = array.shape
    spot = [jax.random.randint(jax.random.fold_in(own_key, axis), (), 0, dims[axis]) for axis in range(len(dims))]
    array = array.at[tuple(spot)].set(smallest)
    longest = dims.index(max(dims))
    spot[longest] = (spot[longest] + 1) % dims[longest]
    return array.at[tuple(spot)].set(high)


def block_scale(stream_key, shape, shards, smallest, high):
    def one(position, blocks):
        heights = jax.random.uniform(jax.random.fold_in(jax.random.fold_in(stream_key, 6), position), (blocks,), jnp.float32, smallest / len(shards), high / len(shards))
        return jnp.repeat(jnp.exp(heights), shape[position] // blocks).reshape((-1,) + (1,) * (len(shape) - position - 1))

    loudness = one(*shards[0])
    for cut in shards[1:]:
        loudness = loudness * one(*cut)
    return loudness


def normal_values(own_key, extent, width, bound, cuts=(), held_as=jnp.bfloat16):
    result = jax.random.normal(own_key, extent, jnp.float32) * width
    if len(cuts) > 0:
        result = block_scale(own_key, extent, cuts, -0.22, 0.18) * result
    return jnp.clip(result, min=-bound, max=bound).astype(held_as)


def setup_inputs(seed: int = 0, part: int = 0) -> dict:
    key_of = jax.random.split(jax.random.key(seed), 9)
    part_keys = jax.random.split(jax.random.fold_in(key_of[8], part), 9)
    estimate = normal_values(part_keys[0], (2, NZ, NY, NX), 1.0, 6.0, ((1, 8), (2, 2)), jnp.float32)
    coil_sens = normal_values(part_keys[1], (2, NCOIL, NZ, NY, NX), 0.5, 3.0, ((1, 2), (2, 8)))
    measured = normal_values(part_keys[2], (2, NCOIL, NZ, NY, NX), 0.7, 4.1875, ((1, 2), (3, 8)))
    sampling = set_ends((jax.random.randint(part_keys[3], (NZ, NY), 0, 3) < 1).astype(jnp.int32), jax.random.fold_in(part_keys[3], 1), 0, 1)
    step_size = jnp.clip(jax.random.uniform(key_of[4], (1,), jnp.float32, 0.2, 2.0), 0.2, 2.0)
    conv_in = normal_values(key_of[5], (HID, 2, 3, 3, 3), 54 ** -0.5, 0.875)
    bias_in = normal_values(key_of[6], (HID,), 0.5, 3.0, (), jnp.float32)
    conv_out = normal_values(key_of[7], (2, HID, 3, 3, 3), (HID * 27) ** -0.5, 0.21875)
    return {"estimate": estimate, "coil_sens": coil_sens, "measured": measured, "sampling": sampling, "step_size": step_size, "conv_in": conv_in, "bias_in": bias_in, "conv_out": conv_out}


PRECISE = lax.Precision.HIGHEST


def leaky_relu(values):
    return jnp.where(values > 0, values, 0.2 * values)


def convolve(volume, kernel):
    return lax.conv_general_dilated(volume[None], kernel, (1, 1, 1), "SAME", dimension_numbers=("NCDHW", "OIDHW", "NCDHW"), precision=PRECISE, preferred_element_type=volume.dtype)[0]


def reference(estimate, coil_sens, measured, sampling, step_size, conv_in, bias_in, conv_out):
    float_type = estimate.dtype
    current = estimate[0] + 1j * estimate[1]
    weights = sampling.astype(float_type)[:, :, None]

    def per_coil(running, pieces):
        coil_map, observed = pieces
        coil_map = coil_map.astype(float_type)
        observed = observed.astype(float_type)
        complex_map = coil_map[0] + 1j * coil_map[1]
        spectrum = jnp.fft.fftn(complex_map * current, norm="ortho")
        misfit = weights * (spectrum - (observed[0] + 1j * observed[1]))
        returned = jnp.fft.ifftn(misfit, norm="ortho")
        return running + jnp.conj(complex_map) * returned, None

    initial = jnp.zeros(current.shape, current.dtype)
    running, _ = lax.scan(per_coil, initial, (jnp.moveaxis(coil_sens, 1, 0), jnp.moveaxis(measured, 1, 0)))
    gradient = jnp.stack([jnp.real(running), jnp.imag(running)]).astype(float_type)
    rounded = lax.optimization_barrier(estimate.astype(jnp.bfloat16)).astype(float_type)
    hidden = leaky_relu(convolve(rounded, conv_in.astype(float_type)) + bias_in.astype(float_type)[:, None, None, None])
    hidden = lax.optimization_barrier(hidden.astype(jnp.bfloat16)).astype(float_type)
    regular = convolve(hidden, conv_out.astype(float_type))
    return estimate - step_size[0] * gradient - regular
```

```python
import functools
import math

import jax
import jax.numpy as jnp
import numpy as np
from jax import lax
from jax.experimental import pallas as pl
from jax.experimental.pallas import tpu as pltpu
from jax.sharding import PartitionSpec as P

LINE = ("slab", "pencil")
HALF = jnp.float16
F32 = jnp.float32
BF16 = jnp.bfloat16
SCALE = 1.0 / 16.0


def line_dft(n):
    k = np.arange(n)
    angles = 2.0 * np.pi * (k[:, None] * k[None, :] % n) / n
    c, s = np.cos(angles) / math.sqrt(n), np.sin(angles) / math.sqrt(n)
    return np.block([[c, s], [-s, c]])


def split(table):
    high = table.astype(BF16)
    low = (table - high.astype(np.float64)).astype(BF16)
    return np.stack([high, low])


def dot(a, b):
    return jnp.dot(a, b, preferred_element_type=F32)


def dot3(table, data):
    high = data.astype(BF16)
    low = (data - high.astype(F32)).astype(BF16)
    return dot(table[0], high) + dot(table[1], high) + dot(table[0], low)


def forward_y_kernel(place_ref, own_ref, other_ref, sens_ref, table_ref, out_ref):
    first = place_ref[0] == 0
    zl = own_ref.shape[1]
    blocks = out_ref.shape[0]
    kyl = out_ref.shape[3] // zl
    n = 2 * own_ref.shape[2]
    table = (table_ref[0], table_ref[1])

    def image(z):
        parts = []
        for ri in range(2):
            own, other = own_ref[ri, z], other_ref[ri, z].astype(F32)
            top = jnp.where(first, own, other)
            bottom = jnp.where(first, other, own)
            parts.append(jnp.concatenate([top, bottom], axis=0))
        sr, si = sens_ref[0, 0, z].astype(F32), sens_ref[1, 0, z].astype(F32)
        re = sr * parts[0] - si * parts[1]
        im = sr * parts[1] + si * parts[0]
        return jnp.concatenate([re, im], axis=0)

    def step(p, carry):
        data = jnp.concatenate([image(2 * p), image(2 * p + 1)], axis=1)
        result = dot3(table, data)
        x = result.shape[1] // 2
        for half in range(2):
            for d in range(blocks):
                for ro in range(2):
                    rows = result[ro * n + d * kyl : ro * n + (d + 1) * kyl, half * x : (half + 1) * x]
                    out_ref[d, 0, ro, pl.ds(2 * p + half, kyl, stride=zl), :] = rows
        return carry

    lax.fori_loop(0, zl // 2, step, 0)


def forward_y(place, own, other, sens, table, blocks):
    _, nc, zl, n, x = sens.shape
    kyl = n // blocks
    return pl.pallas_call(
        forward_y_kernel,
        grid=(nc,),
        in_specs=[
            pl.BlockSpec(memory_space=pltpu.SMEM),
            pl.BlockSpec(own.shape, lambda c: (0, 0, 0, 0)),
            pl.BlockSpec(other.shape, lambda c: (0, 0, 0, 0)),
            pl.BlockSpec((2, 1, zl, n, x), lambda c: (0, c, 0, 0, 0)),
            pl.BlockSpec(table.shape, lambda c: (0, 0, 0)),
        ],
        out_specs=pl.BlockSpec((blocks, 1, 2, kyl * zl, x), lambda c: (0, c, 0, 0, 0)),
        out_shape=jax.ShapeDtypeStruct((blocks, nc, 2, kyl * zl, x), F32),
        cost_estimate=pl.CostEstimate(
            flops=2 * 3 * 2 * n * 2 * n * nc * zl * x, bytes_accessed=14 * sens.size // 2, transcendentals=0
        ),
        name="forward_y",
    )(place, own, other, sens, table)


def middle_kernel(in_ref, circ_ref, meas_ref, out_ref):
    blocks, nc = in_ref.shape[0], in_ref.shape[1]
    kys = circ_ref.shape[1]
    zl = in_ref.shape[3] // kys
    x = in_ref.shape[4]
    n = blocks * zl
    for k in range(kys):
        columns = []
        for c in range(nc):
            rows = [in_ref[s, c, ri, k * zl : (k + 1) * zl, :] for ri in range(2) for s in range(blocks)]
            columns.append(jnp.concatenate(rows, axis=0))
        data = jnp.concatenate(columns, axis=1)
        result = dot3((circ_ref[0, k], circ_ref[1, k]), data) - meas_ref[k]
        for c in range(nc):
            for ri in range(2):
                for d in range(blocks):
                    out_ref[d, c, ri, k * zl : (k + 1) * zl, :] = result[
                        ri * n + d * zl : ri * n + (d + 1) * zl, c * x : (c + 1) * x
                    ]


def middle(data, circ, meas):
    blocks, nc, _, rows, x = data.shape
    kyl, n2 = circ.shape[1], circ.shape[2]
    zl = rows // kyl
    kb = 2
    block = (blocks, nc, 2, kb * zl, x)
    return pl.pallas_call(
        middle_kernel,
        grid=(kyl // kb,),
        in_specs=[
            pl.BlockSpec(block, lambda k: (0, 0, 0, k, 0)),
            pl.BlockSpec((2, kb, n2, n2), lambda k: (0, k, 0, 0)),
            pl.BlockSpec((kb, n2, nc * x), lambda k: (k, 0, 0)),
        ],
        out_specs=pl.BlockSpec(block, lambda k: (0, 0, 0, k, 0)),
        out_shape=jax.ShapeDtypeStruct(data.shape, F32),
        cost_estimate=pl.CostEstimate(
            flops=2 * 3 * n2 * n2 * kyl * nc * x, bytes_accessed=12 * data.size, transcendentals=0
        ),
        name="middle_z",
    )(data, circ, meas)


def backward_y_kernel(in_ref, sens_ref, table_ref, out_ref):
    blocks = in_ref.shape[0]
    zl = out_ref.shape[1]
    n, x = out_ref.shape[2], out_ref.shape[3]
    kyl = n // blocks
    table = (table_ref[0], table_ref[1])

    @pl.when(pl.program_id(0) == 0)
    def _():
        out_ref[...] = jnp.zeros_like(out_ref)

    def step(p, carry):
        columns = []
        for half in range(2):
            rows = [
                in_ref[s, 0, ri, pl.ds(2 * p + half, kyl, stride=zl), :] for ri in range(2) for s in range(blocks)
            ]
            columns.append(jnp.concatenate(rows, axis=0))
        result = dot3(table, jnp.concatenate(columns, axis=1))
        for half in range(2):
            z = 2 * p + half
            cr = result[:n, half * x : (half + 1) * x]
            ci = result[n:, half * x : (half + 1) * x]
            sr, si = sens_ref[0, 0, z].astype(F32), sens_ref[1, 0, z].astype(F32)
            out_ref[0, z] += sr * cr + si * ci
            out_ref[1, z] += sr * ci - si * cr
        return carry

    lax.fori_loop(0, zl // 2, step, 0)


def backward_y(data, sens, table):
    _, nc, zl, n, x = sens.shape
    blocks = data.shape[0]
    return pl.pallas_call(
        backward_y_kernel,
        grid=(nc,),
        in_specs=[
            pl.BlockSpec((blocks, 1, 2, data.shape[3], x), lambda c: (0, c, 0, 0, 0)),
            pl.BlockSpec((2, 1, zl, n, x), lambda c: (0, c, 0, 0, 0)),
            pl.BlockSpec(table.shape, lambda c: (0, 0, 0)),
        ],
        out_specs=pl.BlockSpec((2, zl, n, x), lambda c: (0, 0, 0, 0)),
        out_shape=jax.ShapeDtypeStruct((2, zl, n, x), F32),
        cost_estimate=pl.CostEstimate(
            flops=2 * 3 * 2 * n * 2 * n * nc * zl * x, bytes_accessed=14 * sens.size // 2, transcendentals=0
        ),
        name="backward_y",
    )(data, sens, table)


def measured_images(measured, sampling, table_z, table_x):
    _, nc, nz, kyl, nx = measured.shape
    masked = jnp.where((sampling > 0)[None, None, :, :, None], measured, 0).astype(BF16)
    tx = table_x.reshape(2, 2, nx, 2, nx)
    form = "pfqx,pczkf->kqzcx"
    along_x = jnp.einsum(form, tx[0], masked, preferred_element_type=F32)
    along_x = along_x + jnp.einsum(form, tx[1], masked, preferred_element_type=F32)
    high = lax.reduce_precision(along_x, 8, 7)
    low = (along_x - high).astype(BF16)
    high = high.astype(BF16)
    stacked = jnp.stack([high, low])
    tz = table_z.reshape(2, 2, nz, 2, nz)
    tz = jnp.stack([tz[0], tz[0], tz[1]])
    stacked = jnp.stack([high, low, high])
    out = jnp.einsum("tpzqw,tkpzcx->kqwcx", tz, stacked, preferred_element_type=F32)
    return out.reshape(kyl, 2 * nz, nc * nx)


def circulants(sampling, table_z):
    nz = sampling.shape[0]
    weights = (sampling > 0).astype(BF16).T
    weights = jnp.concatenate([weights, weights], axis=1)
    left = jnp.concatenate([table_z[0], table_z[1], table_z[0]], axis=0)
    right = jnp.concatenate([table_z[0], table_z[0], table_z[1]], axis=0)
    scaled = right[None] * jnp.tile(weights, (1, 3))[:, :, None]
    circ = jnp.einsum("kw,ykz->ywz", left, scaled, preferred_element_type=F32)
    high = lax.reduce_precision(circ, 8, 7)
    return jnp.stack([high.astype(BF16), (circ - high).astype(BF16)])


def conv_kernel(edge_ref, frame_ref, w1_ref, w2_ref, bias_ref, out_ref, cols_ref, acc_ref, *, nyb, hid):
    planes = frame_ref.shape[1]
    x = frame_ref.shape[3]
    rows = cols_ref.shape[0] // planes
    lane = lax.broadcasted_iota(jnp.int32, (24, x), 1)
    acc_ref[...] = jnp.zeros_like(acc_ref)

    def gather(z, carry):
        pieces = []
        for c in range(2):
            blocks = [frame_ref[c, z, yb * 16 : yb * 16 + 24, :] for yb in range(nyb)]
            for d in range(3):
                if d == 0:
                    moved = [jnp.where(lane == 0, 0.0, pltpu.roll(b, 1, 1)) for b in blocks]
                elif d == 2:
                    moved = [jnp.where(lane == x - 1, 0.0, pltpu.roll(b, x - 1, 1)) for b in blocks]
                else:
                    moved = blocks
                pieces.append(jnp.concatenate(moved, axis=1))
        cols_ref[pl.ds(pl.multiple_of(z * rows, 16), rows), :] = jnp.concatenate(pieces, axis=0).astype(BF16)
        return carry

    lax.fori_loop(0, planes, gather, 0)
    lane16 = lax.broadcasted_iota(jnp.int32, (32, x), 1)

    def plane(z, carry):
        cols = cols_ref[pl.ds(pl.multiple_of(z * rows, 16), 3 * rows), :]
        hidden = dot(w1_ref[...], cols)
        hidden = hidden + jnp.concatenate([bias_ref[...]] * nyb, axis=1)
        hidden = jnp.where(hidden > 0, hidden, 0.2 * hidden)
        top = hidden[:hid] * jnp.concatenate(
            [jnp.full((hid, x), edge_ref[0], F32)] + [jnp.ones((hid, x), F32)] * (nyb - 1), axis=1
        )
        bottom = hidden[-hid:] * jnp.concatenate(
            [jnp.ones((hid, x), F32)] * (nyb - 1) + [jnp.full((hid, x), edge_ref[1], F32)], axis=1
        )
        hidden = jnp.concatenate([top, hidden[hid:-hid], bottom], axis=0).astype(BF16)
        products = dot(w2_ref[...], hidden)
        z_global = edge_ref[2] + z
        keep = jnp.where((z_global >= 0) & (z_global < edge_ref[3]), 1, 0).astype(F32)
        for a in range(3):
            for yb in range(nyb):
                p = [products[(a * 3 + d) * 32 : (a * 3 + d + 1) * 32, yb * x : (yb + 1) * x] for d in range(3)]
                total = (
                    p[1]
                    + jnp.where(lane16 == 0, 0.0, pltpu.roll(p[0], 1, 1))
                    + jnp.where(lane16 == x - 1, 0.0, pltpu.roll(p[2], x - 1, 1))
                )
                acc_ref[z + 2 - a, :, yb * x : (yb + 1) * x] += keep * total
        return carry

    lax.fori_loop(0, planes - 2, plane, 0)

    def emit(z, carry):
        for q in range(2):
            for yb in range(nyb):
                out_ref[q, z, yb * 16 : (yb + 1) * 16, :] = acc_ref[z + 2, q * 16 : (q + 1) * 16, yb * x : (yb + 1) * x]
        return carry

    lax.fori_loop(0, out_ref.shape[1], emit, 0)


def band_weights(conv_in, conv_out):
    hid = conv_in.shape[0]
    shift = np.arange(3)
    w = jnp.transpose(conv_in, (3, 0, 2, 1, 4)).reshape(3, hid, 18)
    spread = np.repeat(np.eye(18), 24, axis=1).astype(BF16)
    wide = jnp.einsum("bok,kl->bol", w, spread, preferred_element_type=F32)
    hit = np.arange(18)[None, :, None] + shift[:, None, None] == np.arange(24)[None, None, :]
    hit = np.tile(hit, (1, 1, 18)).astype(np.float32)
    w1 = jnp.sum(wide[:, None] * hit[:, :, None, :], axis=0).astype(BF16).reshape(18 * hid, 18 * 24)
    v = jnp.transpose(conv_out, (3, 2, 4, 0, 1)).reshape(3, 18, hid)
    spread = np.tile(np.eye(hid), (1, 18)).astype(BF16)
    wide = jnp.einsum("bko,ol->bkl", v, spread, preferred_element_type=F32)
    hit = np.arange(16)[None, :, None] + shift[:, None, None] == np.arange(18)[None, None, :]
    hit = np.repeat(hit, hid, axis=2).astype(np.float32)
    w2 = jnp.sum(wide[:, :, None] * hit[:, None], axis=0).astype(BF16).reshape(18 * 16, 18 * hid)
    return w1, w2


def regularizer(framed, conv_in, bias_in, conv_out, size_z):
    hid = conv_in.shape[0]
    _, planes, yframe, x = framed.shape
    zl, yl = planes - 4, yframe - 4
    nyb = yl // 16
    w1, w2 = band_weights(conv_in, conv_out)
    bias = jnp.broadcast_to(jnp.tile(bias_in, 18)[:, None], (18 * hid, x))
    frame = jnp.pad(framed.astype(F32), ((0, 0), (0, 0), (0, 4), (0, 0)))
    last = lax.axis_size("coil") - 1
    at = lax.axis_index("coil")
    edges = jnp.stack(
        [
            (at > 0).astype(jnp.int32),
            (at < last).astype(jnp.int32),
            (lax.axis_index(LINE) * zl - 1).astype(jnp.int32),
            jnp.int32(size_z),
        ]
    )
    vmem = pl.BlockSpec(memory_space=pltpu.VMEM)
    return pl.pallas_call(
        functools.partial(conv_kernel, nyb=nyb, hid=hid),
        in_specs=[pl.BlockSpec(memory_space=pltpu.SMEM)] + [vmem] * 4,
        out_specs=vmem,
        out_shape=jax.ShapeDtypeStruct((2, zl, yl, x), F32),
        scratch_shapes=[
            pltpu.VMEM((planes * 144, nyb * x), BF16),
            pltpu.VMEM((zl + 4, 32, nyb * x), F32),
        ],
        cost_estimate=pl.CostEstimate(
            flops=2 * (zl + 2) * nyb * x * (576 * 432 + 288 * 576), bytes_accessed=4 << 20, transcendentals=0
        ),
        name="regularizer",
    )(edges, frame, w1, w2, bias)


def extended(x, sides, width):
    for axis, dim in sides:
        size, length = (lax.axis_size(axis), x.shape[dim])
        up = [(i, (i + 1) % size) for i in range(size - 1)]
        down = [(j, i) for i, j in up]
        last = lax.slice_in_dim(x, length - width, length, axis=dim)
        initial = lax.slice_in_dim(x, 0, width, axis=dim)
        before = lax.ppermute(last, axis, up)
        after = lax.ppermute(initial, axis, down)
        x = jnp.concatenate([before, x, after], axis=dim)
    return x


def fast_body(estimate, coil_sens, measured, sampling, step_size, conv_in, bias_in, conv_out):
    _, nc, zl, ny, nx = coil_sens.shape
    nz = measured.shape[2]
    yl = estimate.shape[2]
    blocks = lax.axis_size(LINE)
    swap = [(0, 1), (1, 0)]
    at = lax.axis_index("coil")
    table_y = jnp.asarray(split(line_dft(ny)))
    table_z = jnp.asarray(split(line_dft(nz)))
    table_x = jnp.asarray(split(line_dft(nx)))
    back_y = jnp.asarray(split(line_dft(ny).T))

    other = lax.ppermute(estimate.astype(HALF), "coil", swap).astype(F32)
    framed = extended(estimate.astype(BF16), ((LINE, 1), ("coil", 2)), 2)
    place = jnp.reshape(at, (1,)).astype(jnp.int32)
    sent = forward_y(place, estimate, other, coil_sens, table_y, blocks)
    lines = lax.all_to_all(sent.astype(HALF), LINE, split_axis=0, concat_axis=0, tiled=True)
    circ = circulants(sampling, table_z)
    meas = measured_images(measured, sampling, table_z, table_x)
    back = middle(lines.astype(F32), circ, meas)
    regular = regularizer(framed, conv_in, bias_in, conv_out, nz)
    slabs = lax.all_to_all(back.astype(HALF), LINE, split_axis=0, concat_axis=0, tiled=True)
    partial = backward_y(slabs.astype(F32), coil_sens, back_y)
    mine = lax.dynamic_slice_in_dim(partial, at * yl, yl, axis=2)
    theirs = lax.dynamic_slice_in_dim(partial, (1 - at) * yl, yl, axis=2)
    received = lax.ppermute((theirs * SCALE).astype(HALF), "coil", swap).astype(F32) * (1.0 / SCALE)
    return estimate - step_size[0] * (mine + received) - regular


PRECISE = lax.Precision.HIGHEST
LETTERS = "abcdefghij"


def dft_table(length):
    indices = jnp.arange(length, dtype=jnp.int32)
    phases = indices[:, None] * indices[None, :] % length
    angles = phases.astype(jnp.float32) * (2.0 * jnp.pi / length)
    factor = 1.0 / jnp.sqrt(jnp.float32(length))
    return jnp.stack([jnp.cos(angles) * factor, jnp.sin(angles) * factor])


def transform(values, axis_pos, inverse):
    tables = dft_table(values.shape[axis_pos])
    rank_count = values.ndim
    source = LETTERS[:rank_count]
    target = source[:axis_pos] + "z" + source[axis_pos + 1 :]
    products_all = jnp.einsum(
        "tz" + source[axis_pos] + "," + source + "->t" + target, tables, values, precision=PRECISE
    )
    cos_real, cos_imag = (products_all[0, 0], products_all[0, 1])
    sin_real, sin_imag = (products_all[1, 0], products_all[1, 1])
    if inverse:
        return jnp.stack([cos_real - sin_imag, cos_imag + sin_real])
    return jnp.stack([cos_real + sin_imag, cos_imag - sin_real])


def complex_product(operand, partner, conjugate):
    if conjugate:
        real_part = operand[0] * partner[0] + operand[1] * partner[1]
        imag_part = operand[0] * partner[1] - operand[1] * partner[0]
    else:
        real_part = operand[0] * partner[0] - operand[1] * partner[1]
        imag_part = operand[0] * partner[1] + operand[1] * partner[0]
    return jnp.stack([real_part, imag_part])


def generic_regularizer(estimate, conv_in, bias_in, conv_out, size_z, size_y):
    hidden_count = conv_in.shape[0]
    z_local, y_local, x_count = (estimate.shape[1], estimate.shape[2], estimate.shape[3])
    plane_input = estimate.astype(jnp.bfloat16)
    rim_depth = 2
    framed = extended(plane_input, ((("slab", "pencil"), 1), ("coil", 2)), rim_depth)
    framed = jnp.pad(framed, ((0, 0), (0, 0), (0, 0), (1, 1)))
    z_out = z_local + 2 * rim_depth - 2
    y_out = y_local + 2 * rim_depth - 2
    columns = jnp.stack(
        [
            framed[
                :, shift_z : shift_z + z_out, shift_y : shift_y + y_out, shift_x : shift_x + x_count
            ]
            for shift_z in range(3)
            for shift_y in range(3)
            for shift_x in range(3)
        ],
        axis=1,
    )
    columns = columns.reshape(2 * 27, z_out * y_out * x_count)
    kernel_in = conv_in.reshape(hidden_count, 2 * 27)
    hidden = jnp.dot(kernel_in, columns, preferred_element_type=jnp.float32) + bias_in[:, None]
    hidden = jnp.where(hidden > 0, hidden, 0.2 * hidden).reshape(
        hidden_count, z_out, y_out, x_count
    )
    z_global = lax.axis_index(("slab", "pencil")) * z_local - 1 + lax.iota(jnp.int32, z_out)
    y_global = lax.axis_index("coil") * y_local - 1 + lax.iota(jnp.int32, y_out)
    inside = ((z_global >= 0) & (z_global < size_z))[:, None] & ((y_global >= 0) & (y_global < size_y))[
        None, :
    ]
    framed_hidden = jnp.where(inside[None, :, :, None], hidden, 0.0).astype(jnp.bfloat16)
    framed_hidden = jnp.pad(framed_hidden, ((0, 0), (0, 0), (0, 0), (1, 1)))
    result = jnp.zeros((2, z_local, y_local, x_count), jnp.float32)
    for shift_z in range(3):
        kernel_plane = jnp.transpose(conv_out[:, :, shift_z], (0, 2, 3, 1)).reshape(
            18, hidden_count
        )
        products = jnp.einsum(
            "qc,czyx->qzyx",
            kernel_plane,
            framed_hidden[:, shift_z : shift_z + z_local],
            preferred_element_type=jnp.float32,
        )
        products = products.reshape(2, 3, 3, z_local, y_local + 2, x_count + 2)
        for shift_y in range(3):
            for shift_x in range(3):
                result = (
                    result
                    + products[
                        :,
                        shift_y,
                        shift_x,
                        :,
                        shift_y : shift_y + y_local,
                        shift_x : shift_x + x_count,
                    ]
                )
    return result


def generic_body(estimate, coil_sens, measured, sampling, step_size, conv_in, bias_in, conv_out):
    gathered = lax.all_gather(estimate, "coil", axis=2, tiled=True)
    coil_maps = coil_sens.astype(jnp.float32)
    coil_images = complex_product(coil_maps, gathered[:, None], False)
    spectra = transform(transform(coil_images, 4, False), 3, False)
    pencils = lax.all_to_all(spectra, ("slab", "pencil"), split_axis=3, concat_axis=2, tiled=True)
    spectra_full = transform(pencils, 2, False)
    weights = sampling.astype(jnp.float32)[None, None, :, :, None]
    misfit = weights * (spectra_full - measured.astype(jnp.float32))
    misfit_back = transform(misfit, 2, True)
    slab_view = lax.all_to_all(
        misfit_back, ("slab", "pencil"), split_axis=2, concat_axis=3, tiled=True
    )
    coil_back = transform(transform(slab_view, 3, True), 4, True)
    partial_terms = jnp.sum(complex_product(coil_maps, coil_back, True), axis=1)
    gradient = lax.psum_scatter(partial_terms, "coil", scatter_dimension=2, tiled=True)
    regular = generic_regularizer(
        estimate, conv_in, bias_in, conv_out, measured.shape[2], coil_sens.shape[3]
    )
    return estimate - step_size[0] * gradient - regular


def body(*arrays):
    estimate, coil_sens = arrays[0], arrays[1]
    _, zl, yl, nx = estimate.shape
    ny = coil_sens.shape[3]
    kyl = ny // lax.axis_size(LINE)
    fits = zl % 16 == 0 and kyl % 16 == 0 and yl % 16 == 0 and nx == 128 and lax.axis_size("coil") == 2
    return fast_body(*arrays) if fits else generic_body(*arrays)


def solution(mesh):
    in_specs = (
        P(None, ("groups", "slab", "pencil"), "coil", None),
        P(None, "coil", ("groups", "slab", "pencil"), None, None),
        P(None, "coil", None, ("groups", "slab", "pencil"), None),
        P(None, ("groups", "slab", "pencil")),
        P(),
        P(),
        P(),
        P(),
    )
    out_specs = P(None, ("groups", "slab", "pencil"), "coil", None)
    return jax.shard_map(body, mesh=mesh, in_specs=in_specs, out_specs=out_specs, check_vma=False)
```

```python
import functools
import math

import jax
import jax.numpy as jnp
import numpy as np
from jax import lax
from jax.experimental import pallas as pl
from jax.experimental.pallas import tpu as pltpu
from jax.sharding import PartitionSpec as P


LINE = ("slab", "pencil")
HALF = jnp.float16
F32 = jnp.float32
BF16 = jnp.bfloat16
SCALE = 1.0 / 16.0
CHUNKS = 2


def line_dft(n):
    k = np.arange(n)
    angles = 2.0 * np.pi * (k[:, None] * k[None, :] % n) / n
    c, s = np.cos(angles) / math.sqrt(n), np.sin(angles) / math.sqrt(n)
    return np.block([[c, s], [-s, c]])


def split(table):
    high = table.astype(BF16)
    low = (table - high.astype(np.float64)).astype(BF16)
    return np.stack([high, low])


def dot(a, b):
    return jnp.dot(a, b, preferred_element_type=F32)


def dot3(table, data):
    high = data.astype(BF16)
    low = (data - high.astype(F32)).astype(BF16)
    return dot(table, jnp.concatenate([high, high, low], axis=0))


def wide(table):
    return jnp.concatenate([table[0], table[1], table[0]], axis=1)


def by_device(table, slabs, cores):
    _, rows, columns = table.shape
    width = rows // (2 * slabs * cores)
    table = jnp.asarray(table).reshape(4, slabs, cores, width, columns)
    for axis, name, size in ((1, "slab", slabs), (2, "pencil", cores)):
        at = lax.axis_index(name)
        for bit in range(size.bit_length() - 1):
            other = np.arange(size) ^ (1 << bit)
            flipped = jnp.concatenate([lax.slice_in_dim(table, o, o + 1, axis=axis) for o in other], axis=axis)
            table = jnp.where((at >> bit) & 1 == 1, flipped, table)
    return table.reshape(2, rows, columns)


def payloads(near, far, slabs):
    got = lax.ppermute(far.astype(HALF), "pencil", [(0, 1), (1, 0)])
    both = [jnp.stack([near[k].astype(HALF), got[k]]) for k in range(slabs - 1, 0, -1)]
    return both, [near, got[0].astype(F32)[None]]


def delivered(both, own, slabs):
    moved = {}
    for k, payload in zip(range(slabs - 1, 0, -1), both):
        moved[k] = lax.ppermute(payload, "slab", [(i, i ^ k) for i in range(slabs)])
        moved[k] = moved[k].astype(F32)
    return own + [moved[k] for k in range(1, slabs)]


def piece_specs(pieces, block, index):
    specs = []
    for k, piece in enumerate(pieces):
        lead = 1 if k < 2 else piece.shape[0]
        specs.append(pl.BlockSpec((lead,) + block, index))
    return specs


def piece_views(refs):
    return [ref.at[lead] for ref in refs for lead in range(ref.shape[0])]


def forward_y_kernel(place_ref, own_ref, other_ref, sens_ref, table_ref, near_ref, far_ref):
    first = place_ref[0] == 0
    zl = own_ref.shape[1]
    slabs = near_ref.shape[0]
    kyl = near_ref.shape[3] // zl
    n = 2 * own_ref.shape[2]
    table = table_ref[...]

    def image(z):
        parts = []
        for ri in range(2):
            own, other = own_ref[ri, z], other_ref[ri, z]
            top = jnp.where(first, own, other)
            bottom = jnp.where(first, other, own)
            parts.append(jnp.concatenate([top, bottom], axis=0))
        sr, si = sens_ref[0, 0, z].astype(F32), sens_ref[1, 0, z].astype(F32)
        re = sr * parts[0] - si * parts[1]
        im = sr * parts[1] + si * parts[0]
        return jnp.concatenate([re, im], axis=0)

    def step(p, carry):
        data = jnp.concatenate([image(2 * p), image(2 * p + 1)], axis=1)
        result = dot3(table, data)
        x = result.shape[1] // 2
        for half in range(2):
            for k in range(slabs):
                for core, ref in enumerate((near_ref, far_ref)):
                    d = 2 * k + core
                    for ro in range(2):
                        rows = result[ro * n + d * kyl : ro * n + (d + 1) * kyl, half * x : (half + 1) * x]
                        ref[k, 0, ro, pl.ds(2 * p + half, kyl, stride=zl), :] = rows
        return carry

    lax.fori_loop(0, zl // 2, step, 0)


def forward_y(place, own, other, sens, table, slabs, first, nc):
    _, _, zl, n, x = sens.shape
    kyl = n // (2 * slabs)
    out = pl.BlockSpec((slabs, 1, 2, kyl * zl, x), lambda c: (0, c, 0, 0, 0))
    return pl.pallas_call(
        forward_y_kernel,
        grid=(nc,),
        in_specs=[
            pl.BlockSpec(memory_space=pltpu.SMEM),
            pl.BlockSpec(own.shape, lambda c: (0, 0, 0, 0)),
            pl.BlockSpec(other.shape, lambda c: (0, 0, 0, 0)),
            pl.BlockSpec((2, 1, zl, n, x), lambda c: (0, first + c if first else c, 0, 0, 0)),
            pl.BlockSpec(table.shape, lambda c: (0, 0)),
        ],
        out_specs=[out, out],
        out_shape=[jax.ShapeDtypeStruct((slabs, nc, 2, kyl * zl, x), F32)] * 2,
        cost_estimate=pl.CostEstimate(
            flops=2 * 3 * 2 * n * 2 * n * nc * zl * x, bytes_accessed=14 * nc * zl * n * x, transcendentals=0
        ),
    )(place, own, other, sens, table)


def middle_kernel(count, *refs):
    pieces = piece_views(refs[:count])
    high_ref, low_ref, meas_ref, near_ref, far_ref = refs[count:]
    nc = pieces[0].shape[0]
    kys = high_ref.shape[0]
    zl = pieces[0].shape[2] // kys
    x = pieces[0].shape[3]
    n = len(pieces) * zl
    for k in range(kys):
        columns = []
        for c in range(nc):
            rows = [piece[c, ri, k * zl : (k + 1) * zl, :] for ri in range(2) for piece in pieces]
            columns.append(jnp.concatenate(rows, axis=0))
        data = jnp.concatenate(columns, axis=1)
        table = jnp.concatenate([high_ref[k], low_ref[k], high_ref[k]], axis=1)
        result = dot3(table, data) - meas_ref[k]
        for c in range(nc):
            for ri in range(2):
                for d in range(len(pieces)):
                    ref = far_ref if d % 2 else near_ref
                    ref[d // 2, c, ri, k * zl : (k + 1) * zl, :] = result[
                        ri * n + d * zl : ri * n + (d + 1) * zl, c * x : (c + 1) * x
                    ]


def middle(pieces, circ, meas):
    _, nc, _, rows, x = pieces[0].shape
    kyl, n2 = circ[0].shape[:2]
    zl = rows // kyl
    slabs = n2 // (4 * zl)
    kb = 2
    out = pl.BlockSpec((slabs, nc, 2, kb * zl, x), lambda k: (0, 0, 0, k, 0))
    return pl.pallas_call(
        functools.partial(middle_kernel, len(pieces)),
        grid=(kyl // kb,),
        in_specs=piece_specs(pieces, (nc, 2, kb * zl, x), lambda k: (0, 0, 0, k, 0))
        + [
            pl.BlockSpec((kb, n2, n2), lambda k: (k, 0, 0)),
            pl.BlockSpec((kb, n2, n2), lambda k: (k, 0, 0)),
            pl.BlockSpec((kb, n2, nc * x), lambda k: (k, 0, 0)),
        ],
        out_specs=[out, out],
        out_shape=[jax.ShapeDtypeStruct((slabs, nc, 2, rows, x), F32)] * 2,
        cost_estimate=pl.CostEstimate(
            flops=2 * 3 * n2 * n2 * kyl * nc * x, bytes_accessed=12 * nc * n2 * kyl * x, transcendentals=0
        ),
    )(*pieces, *circ, meas)


def backward_y_kernel(count, *refs):
    pieces = piece_views(refs[:count])
    sens_ref, table_ref, before_ref, out_ref = refs[count:]
    zl, n, x = out_ref.shape[1:]
    kyl = n // len(pieces)
    table = table_ref[...]

    @pl.when(pl.program_id(0) == 0)
    def _():
        out_ref[...] = before_ref[...]

    def step(p, carry):
        columns = []
        for half in range(2):
            rows = [piece[0, ri, pl.ds(2 * p + half, kyl, stride=zl), :] for ri in range(2) for piece in pieces]
            columns.append(jnp.concatenate(rows, axis=0))
        result = dot3(table, jnp.concatenate(columns, axis=1))
        for half in range(2):
            z = 2 * p + half
            cr = result[:n, half * x : (half + 1) * x]
            ci = result[n:, half * x : (half + 1) * x]
            sr, si = sens_ref[0, 0, z].astype(F32), sens_ref[1, 0, z].astype(F32)
            out_ref[0, z] += sr * cr + si * ci
            out_ref[1, z] += sr * ci - si * cr
        return carry

    lax.fori_loop(0, zl // 2, step, 0)


def backward_y(pieces, sens, table, before, first):
    _, _, zl, n, x = sens.shape
    _, nc, _, rows, _ = pieces[0].shape
    whole = pl.BlockSpec((2, zl, n, x), lambda c: (0, 0, 0, 0))
    return pl.pallas_call(
        functools.partial(backward_y_kernel, len(pieces)),
        grid=(nc,),
        in_specs=piece_specs(pieces, (1, 2, rows, x), lambda c: (0, c, 0, 0, 0))
        + [
            pl.BlockSpec((2, 1, zl, n, x), lambda c: (0, first + c if first else c, 0, 0, 0)),
            pl.BlockSpec(table.shape, lambda c: (0, 0)),
            whole,
        ],
        out_specs=whole,
        out_shape=jax.ShapeDtypeStruct((2, zl, n, x), F32),
        input_output_aliases={len(pieces) + 2: 0},
        cost_estimate=pl.CostEstimate(
            flops=2 * 3 * 2 * n * 2 * n * nc * zl * x, bytes_accessed=14 * nc * zl * n * x, transcendentals=0
        ),
    )(*pieces, sens, table, before)


def measured_kernel(high_ref, low_ref, table_ref, out_ref):
    nc, kys = high_ref.shape[:2]
    for k in range(kys):
        high = jnp.concatenate([high_ref[c, k] for c in range(nc)], axis=1)
        low = jnp.concatenate([low_ref[c, k] for c in range(nc)], axis=1)
        out_ref[k] = dot(table_ref[...], jnp.concatenate([high, high, low], axis=0))


def measured_images(measured, sampling, table_x, back_z, first, nc):
    measured = lax.slice_in_dim(measured, first, first + nc, axis=1)
    _, _, nz, kyl, nx = measured.shape
    masked = jnp.where((sampling > 0)[None, None, :, :, None], measured, 0).astype(BF16)
    tx = jnp.asarray(table_x).reshape(2, 2, nx, 2, nx)
    form = "pfqx,pczkf->ckqzx"
    along_x = jnp.einsum(form, tx[0], masked, preferred_element_type=F32)
    along_x = along_x + jnp.einsum(form, tx[1], masked, preferred_element_type=F32)
    high = lax.reduce_precision(along_x, 8, 7)
    low = (along_x - high).astype(BF16).reshape(nc, kyl, 2 * nz, nx)
    high = high.astype(BF16).reshape(nc, kyl, 2 * nz, nx)
    kb = 2
    block = pl.BlockSpec((nc, kb, 2 * nz, nx), lambda k: (0, k, 0, 0))
    return pl.pallas_call(
        measured_kernel,
        grid=(kyl // kb,),
        in_specs=[block, block, pl.BlockSpec(back_z.shape, lambda k: (0, 0))],
        out_specs=pl.BlockSpec((kb, 2 * nz, nc * nx), lambda k: (k, 0, 0)),
        out_shape=jax.ShapeDtypeStruct((kyl, 2 * nz, nc * nx), F32),
        cost_estimate=pl.CostEstimate(
            flops=2 * 3 * 4 * nz * nz * kyl * nc * nx, bytes_accessed=16 * nc * kyl * nz * nx, transcendentals=0
        ),
    )(high, low, back_z)


def circulants(sampling, back_z):
    weights = (sampling > 0).astype(BF16).T
    weights = jnp.concatenate([weights, weights], axis=1)
    left = wide(back_z)
    right = jnp.concatenate([back_z[0], back_z[0], back_z[1]], axis=1)
    scaled = right[None] * jnp.tile(weights, (1, 3))[:, None, :]
    circ = jnp.einsum("wk,yzk->ywz", left, scaled, preferred_element_type=F32)
    high = lax.reduce_precision(circ, 8, 7)
    return high.astype(BF16), (circ - high).astype(BF16)


def conv_kernel(edge_ref, frame_ref, w1_ref, w2_ref, bias_ref, out_ref, cols_ref, acc_ref, *, nyb, hid):
    planes = frame_ref.shape[1]
    x = frame_ref.shape[3]
    rows = cols_ref.shape[0] // planes
    lane = lax.broadcasted_iota(jnp.int32, (24, x), 1)
    acc_ref[...] = jnp.zeros_like(acc_ref)

    def gather(z, carry):
        pieces = []
        for c in range(2):
            blocks = [frame_ref[c, z, yb * 16 : yb * 16 + 24, :] for yb in range(nyb)]
            for d in range(3):
                if d == 0:
                    moved = [jnp.where(lane == 0, 0.0, pltpu.roll(b, 1, 1)) for b in blocks]
                elif d == 2:
                    moved = [jnp.where(lane == x - 1, 0.0, pltpu.roll(b, x - 1, 1)) for b in blocks]
                else:
                    moved = blocks
                pieces.append(jnp.concatenate(moved, axis=1))
        cols_ref[pl.ds(pl.multiple_of(z * rows, 16), rows), :] = jnp.concatenate(pieces, axis=0).astype(BF16)
        return carry

    lax.fori_loop(0, planes, gather, 0)
    lane16 = lax.broadcasted_iota(jnp.int32, (32, x), 1)

    def plane(z, carry):
        cols = cols_ref[pl.ds(pl.multiple_of(z * rows, 16), 3 * rows), :]
        hidden = dot(w1_ref[...], cols)
        hidden = hidden + jnp.concatenate([bias_ref[...]] * nyb, axis=1)
        hidden = jnp.where(hidden > 0, hidden, 0.2 * hidden)
        top = hidden[:hid] * jnp.concatenate(
            [jnp.full((hid, x), edge_ref[0], F32)] + [jnp.ones((hid, x), F32)] * (nyb - 1), axis=1
        )
        bottom = hidden[-hid:] * jnp.concatenate(
            [jnp.ones((hid, x), F32)] * (nyb - 1) + [jnp.full((hid, x), edge_ref[1], F32)], axis=1
        )
        hidden = jnp.concatenate([top, hidden[hid:-hid], bottom], axis=0).astype(BF16)
        products = dot(w2_ref[...], hidden)
        z_global = edge_ref[2] + z
        keep = jnp.where((z_global >= 0) & (z_global < edge_ref[3]), 1, 0).astype(F32)
        for a in range(3):
            for yb in range(nyb):
                p = [products[(a * 3 + d) * 32 : (a * 3 + d + 1) * 32, yb * x : (yb + 1) * x] for d in range(3)]
                total = (
                    p[1]
                    + jnp.where(lane16 == 0, 0.0, pltpu.roll(p[0], 1, 1))
                    + jnp.where(lane16 == x - 1, 0.0, pltpu.roll(p[2], x - 1, 1))
                )
                acc_ref[z + 2 - a, :, yb * x : (yb + 1) * x] += keep * total
        return carry

    lax.fori_loop(0, planes - 2, plane, 0)

    def emit(z, carry):
        for q in range(2):
            for yb in range(nyb):
                out_ref[q, z, yb * 16 : (yb + 1) * 16, :] = acc_ref[z + 2, q * 16 : (q + 1) * 16, yb * x : (yb + 1) * x]
        return carry

    lax.fori_loop(0, out_ref.shape[1], emit, 0)


def band_weights(conv_in, conv_out):
    hid = conv_in.shape[0]
    shift = np.arange(3)
    w = jnp.transpose(conv_in, (3, 0, 2, 1, 4)).reshape(3, hid, 18)
    spread = np.repeat(np.eye(18), 24, axis=1).astype(BF16)
    wide = jnp.einsum("bok,kl->bol", w, spread, preferred_element_type=F32)
    hit = np.arange(18)[None, :, None] + shift[:, None, None] == np.arange(24)[None, None, :]
    hit = np.tile(hit, (1, 1, 18)).astype(np.float32)
    w1 = jnp.sum(wide[:, None] * hit[:, :, None, :], axis=0).astype(BF16).reshape(18 * hid, 18 * 24)
    v = jnp.transpose(conv_out, (3, 2, 4, 0, 1)).reshape(3, 18, hid)
    spread = np.tile(np.eye(hid), (1, 18)).astype(BF16)
    wide = jnp.einsum("bko,ol->bkl", v, spread, preferred_element_type=F32)
    hit = np.arange(16)[None, :, None] + shift[:, None, None] == np.arange(18)[None, None, :]
    hit = np.repeat(hit, hid, axis=2).astype(np.float32)
    w2 = jnp.sum(wide[:, :, None] * hit[:, None], axis=0).astype(BF16).reshape(18 * 16, 18 * hid)
    return w1, w2


def regularizer(framed, conv_in, bias_in, conv_out, size_z):
    hid = conv_in.shape[0]
    _, planes, yframe, x = framed.shape
    zl, yl = planes - 4, yframe - 4
    nyb = yl // 16
    w1, w2 = band_weights(conv_in, conv_out)
    bias = jnp.broadcast_to(jnp.tile(bias_in, 18)[:, None], (18 * hid, x))
    frame = jnp.pad(framed.astype(F32), ((0, 0), (0, 0), (0, 4), (0, 0)))
    last = lax.axis_size("coil") - 1
    at = lax.axis_index("coil")
    edges = jnp.stack(
        [
            (at > 0).astype(jnp.int32),
            (at < last).astype(jnp.int32),
            (lax.axis_index(LINE) * zl - 1).astype(jnp.int32),
            jnp.int32(size_z),
        ]
    )
    vmem = pl.BlockSpec(memory_space=pltpu.VMEM)
    return pl.pallas_call(
        functools.partial(conv_kernel, nyb=nyb, hid=hid),
        in_specs=[pl.BlockSpec(memory_space=pltpu.SMEM)] + [vmem] * 4,
        out_specs=vmem,
        out_shape=jax.ShapeDtypeStruct((2, zl, yl, x), F32),
        scratch_shapes=[
            pltpu.VMEM((planes * 144, nyb * x), BF16),
            pltpu.VMEM((zl + 4, 32, nyb * x), F32),
        ],
        cost_estimate=pl.CostEstimate(
            flops=2 * (zl + 2) * nyb * x * (576 * 432 + 288 * 576), bytes_accessed=4 << 20, transcendentals=0
        ),
        name="regularizer",
    )(edges, frame, w1, w2, bias)


def extended(x, sides, width):
    for axis, dim in sides:
        size, length = (lax.axis_size(axis), x.shape[dim])
        up = [(i, (i + 1) % size) for i in range(size - 1)]
        down = [(j, i) for i, j in up]
        last = lax.slice_in_dim(x, length - width, length, axis=dim)
        initial = lax.slice_in_dim(x, 0, width, axis=dim)
        before = lax.ppermute(last, axis, up)
        after = lax.ppermute(initial, axis, down)
        x = jnp.concatenate([before, x, after], axis=dim)
    return x


def fast_body(estimate, coil_sens, measured, sampling, step_size, conv_in, bias_in, conv_out):
    _, nc, zl, ny, nx = coil_sens.shape
    nz = measured.shape[2]
    yl = estimate.shape[2]
    slabs, cores = lax.axis_size("slab"), lax.axis_size("pencil")
    swap = [(0, 1), (1, 0)]
    at = lax.axis_index("coil")
    table_y = by_device(split(line_dft(ny)), slabs, cores)
    back_y = wide(jnp.swapaxes(table_y, 1, 2))
    table_y = wide(table_y)
    back_z = by_device(split(line_dft(nz).T), slabs, cores)
    table_x = split(line_dft(nx))

    rounded = estimate.astype(BF16)
    facing = jnp.where(at == 0, rounded[:, :, yl - 2 :], rounded[:, :, :2])
    payload = jnp.concatenate([estimate.astype(HALF), facing.astype(HALF)], axis=2)
    payload = lax.ppermute(payload, "coil", swap)
    other = payload[:, :, :yl].astype(F32)
    facing = payload[:, :, yl:].astype(BF16)
    none = jnp.zeros_like(facing)
    framed = jnp.concatenate(
        [jnp.where(at == 0, none, facing), rounded, jnp.where(at == 0, facing, none)], axis=2
    )

    place = jnp.reshape(at, (1,)).astype(jnp.int32)

    def after(value, *others):
        return lax.optimization_barrier((value,) + others)[0]

    starts = [(first, nc // CHUNKS) for first in range(0, nc, nc // CHUNKS)]
    lines, mine = [], estimate
    for f, n in starts:
        sent = forward_y(place, mine, other, coil_sens, table_y, slabs, f, n)
        both, own = payloads(*sent, slabs)
        mine = after(mine, both)
        lines.append(delivered(both, own, slabs))
    measured, sampling, framed, conv_in, conv_out = lax.optimization_barrier(
        (measured, sampling, framed, conv_in, conv_out, mine)
    )[:5]
    framed = extended(framed, ((LINE, 1),), 2)
    circ = circulants(sampling, back_z)
    back_z = wide(back_z)
    meas = {}
    for f, n in starts:
        meas[f] = measured_images(measured, sampling, table_x, back_z, f, n)
    slices = []
    for pieces, (f, n) in zip(lines, starts):
        both = middle(pieces, circ, meas[f])
        both, own = payloads(*both, slabs)
        slices.append(delivered(both, own, slabs))
    regular = regularizer(framed, conv_in, bias_in, conv_out, nz)
    partial = jnp.zeros((2, zl, ny, nx), F32)
    for pieces, (f, n) in zip(slices, starts):
        partial = backward_y(pieces, coil_sens, back_y, partial, f)
    mine = lax.dynamic_slice_in_dim(partial, at * yl, yl, axis=2)
    theirs = lax.dynamic_slice_in_dim(partial, (1 - at) * yl, yl, axis=2)
    received = lax.ppermute((theirs * SCALE).astype(HALF), "coil", swap).astype(F32) * (1.0 / SCALE)
    return estimate - step_size[0] * (mine + received) - regular


PRECISE = lax.Precision.HIGHEST
LETTERS = "abcdefghij"


def dft_table(length):
    indices = jnp.arange(length, dtype=jnp.int32)
    phases = indices[:, None] * indices[None, :] % length
    angles = phases.astype(jnp.float32) * (2.0 * jnp.pi / length)
    factor = 1.0 / jnp.sqrt(jnp.float32(length))
    return jnp.stack([jnp.cos(angles) * factor, jnp.sin(angles) * factor])


def transform(values, axis_pos, inverse):
    tables = dft_table(values.shape[axis_pos])
    rank_count = values.ndim
    source = LETTERS[:rank_count]
    target = source[:axis_pos] + "z" + source[axis_pos + 1 :]
    products_all = jnp.einsum(
        "tz" + source[axis_pos] + "," + source + "->t" + target, tables, values, precision=PRECISE
    )
    cos_real, cos_imag = (products_all[0, 0], products_all[0, 1])
    sin_real, sin_imag = (products_all[1, 0], products_all[1, 1])
    if inverse:
        return jnp.stack([cos_real - sin_imag, cos_imag + sin_real])
    return jnp.stack([cos_real + sin_imag, cos_imag - sin_real])


def complex_product(operand, partner, conjugate):
    if conjugate:
        real_part = operand[0] * partner[0] + operand[1] * partner[1]
        imag_part = operand[0] * partner[1] - operand[1] * partner[0]
    else:
        real_part = operand[0] * partner[0] - operand[1] * partner[1]
        imag_part = operand[0] * partner[1] + operand[1] * partner[0]
    return jnp.stack([real_part, imag_part])


def generic_regularizer(estimate, conv_in, bias_in, conv_out, size_z, size_y):
    hidden_count = conv_in.shape[0]
    z_local, y_local, x_count = (estimate.shape[1], estimate.shape[2], estimate.shape[3])
    plane_input = estimate.astype(jnp.bfloat16)
    rim_depth = 2
    framed = extended(plane_input, ((("slab", "pencil"), 1), ("coil", 2)), rim_depth)
    framed = jnp.pad(framed, ((0, 0), (0, 0), (0, 0), (1, 1)))
    z_out = z_local + 2 * rim_depth - 2
    y_out = y_local + 2 * rim_depth - 2
    columns = jnp.stack(
        [
            framed[
                :, shift_z : shift_z + z_out, shift_y : shift_y + y_out, shift_x : shift_x + x_count
            ]
            for shift_z in range(3)
            for shift_y in range(3)
            for shift_x in range(3)
        ],
        axis=1,
    )
    columns = columns.reshape(2 * 27, z_out * y_out * x_count)
    kernel_in = conv_in.reshape(hidden_count, 2 * 27)
    hidden = jnp.dot(kernel_in, columns, preferred_element_type=jnp.float32) + bias_in[:, None]
    hidden = jnp.where(hidden > 0, hidden, 0.2 * hidden).reshape(
        hidden_count, z_out, y_out, x_count
    )
    z_global = lax.axis_index(("slab", "pencil")) * z_local - 1 + lax.iota(jnp.int32, z_out)
    y_global = lax.axis_index("coil") * y_local - 1 + lax.iota(jnp.int32, y_out)
    inside = ((z_global >= 0) & (z_global < size_z))[:, None] & ((y_global >= 0) & (y_global < size_y))[
        None, :
    ]
    framed_hidden = jnp.where(inside[None, :, :, None], hidden, 0.0).astype(jnp.bfloat16)
    framed_hidden = jnp.pad(framed_hidden, ((0, 0), (0, 0), (0, 0), (1, 1)))
    result = jnp.zeros((2, z_local, y_local, x_count), jnp.float32)
    for shift_z in range(3):
        kernel_plane = jnp.transpose(conv_out[:, :, shift_z], (0, 2, 3, 1)).reshape(
            18, hidden_count
        )
        products = jnp.einsum(
            "qc,czyx->qzyx",
            kernel_plane,
            framed_hidden[:, shift_z : shift_z + z_local],
            preferred_element_type=jnp.float32,
        )
        products = products.reshape(2, 3, 3, z_local, y_local + 2, x_count + 2)
        for shift_y in range(3):
            for shift_x in range(3):
                result = (
                    result
                    + products[
                        :,
                        shift_y,
                        shift_x,
                        :,
                        shift_y : shift_y + y_local,
                        shift_x : shift_x + x_count,
                    ]
                )
    return result


def generic_body(estimate, coil_sens, measured, sampling, step_size, conv_in, bias_in, conv_out):
    gathered = lax.all_gather(estimate, "coil", axis=2, tiled=True)
    coil_maps = coil_sens.astype(jnp.float32)
    coil_images = complex_product(coil_maps, gathered[:, None], False)
    spectra = transform(transform(coil_images, 4, False), 3, False)
    pencils = lax.all_to_all(spectra, ("slab", "pencil"), split_axis=3, concat_axis=2, tiled=True)
    spectra_full = transform(pencils, 2, False)
    weights = sampling.astype(jnp.float32)[None, None, :, :, None]
    misfit = weights * (spectra_full - measured.astype(jnp.float32))
    misfit_back = transform(misfit, 2, True)
    slab_view = lax.all_to_all(
        misfit_back, ("slab", "pencil"), split_axis=2, concat_axis=3, tiled=True
    )
    coil_back = transform(transform(slab_view, 3, True), 4, True)
    partial_terms = jnp.sum(complex_product(coil_maps, coil_back, True), axis=1)
    gradient = lax.psum_scatter(partial_terms, "coil", scatter_dimension=2, tiled=True)
    regular = generic_regularizer(
        estimate, conv_in, bias_in, conv_out, measured.shape[2], coil_sens.shape[3]
    )
    return estimate - step_size[0] * gradient - regular


def body(*arrays):
    estimate, coil_sens = arrays[0], arrays[1]
    _, zl, yl, nx = estimate.shape
    nc, ny = coil_sens.shape[1], coil_sens.shape[3]
    slabs = lax.axis_size("slab")
    fits = (
        nc % CHUNKS == 0
        and nx == 128
        and not (zl % 16 or yl % 16 or ny // lax.axis_size(LINE) % 16)
        and slabs & (slabs - 1) == 0
        and lax.axis_size("pencil") == 2
        and lax.axis_size("coil") == 2
    )
    if not fits:
        return generic_body(*arrays)
    return fast_body(*arrays)


def solution(mesh):
    in_specs = (
        P(None, ("groups", "slab", "pencil"), "coil", None),
        P(None, "coil", ("groups", "slab", "pencil"), None, None),
        P(None, "coil", None, ("groups", "slab", "pencil"), None),
        P(None, ("groups", "slab", "pencil")),
        P(),
        P(),
        P(),
        P(),
    )
    out_specs = P(None, ("groups", "slab", "pencil"), "coil", None)
    return jax.shard_map(body, mesh=mesh, in_specs=in_specs, out_specs=out_specs, check_vma=False)
```
